256 devices in a mesh: ctx: 64 (over x, y, z_hi), head: 4 (over z_lo, core).
Axes of the slice: x: 4, y: 4, z: 8 (z_hi: 4, z_lo: 2; z = z_hi * 2 + z_lo), core: 2. Of those that a mesh axis runs over, the one named last changes fastest.
Arguments:
- queries: bfloat16 [16384, 8192], P('ctx', 'head'), may hold values from -8 to 8
- keys: bfloat16 [16384, 1024], P('ctx', 'head'), may hold values from -6 to 6
- values: bfloat16 [16384, 1024], P('ctx', 'head'), may hold values from -6 to 6
- pass_list: int32 [64, 32], P('ctx'), may hold values from 0 to 127, as said below
- pass_count: int32 [64], P('ctx'), may hold values from 0 to 32, as said below
- final_queries: bfloat16 [64, 8192], P('ctx', 'head'), may hold values from -8 to 8
- final_keys: bfloat16 [64, 1024], P('ctx', 'head'), may hold values from -6 to 6
- final_values: bfloat16 [64, 1024], P('ctx', 'head'), may hold values from -6 to 6
- out_weight: bfloat16 [8192, 8192], P('head', 'ctx'), may hold values from -0.0625 to 0.0625
Outputs:
- attn_out: bfloat16 [16384, 8192], P('ctx', 'head')
- final_out: bfloat16 [64, 8192], P('head', 'ctx')
The draws below stay inside these ranges and needn't reach their ends.
Inputs may be any that keep to these rules, and one draw needn't show every extreme that they name: `pass_list`: the first pass_count[c] entries of row c name blocks of distinct shards, all of shards before c (block b belongs to shard b // 2); the later entries are block numbers that mean nothing. pass_count[c] lies between half of min(32, c), rounded up, and min(32, c); the last shard lists 32 blocks.
All inputs are finite; a program needn't handle non-finite values.
Results may differ from the reference program's by a relative error of at most 0.013.
Values may be sent and summed in bfloat16 or wider, within the bound.
No kernel may reach another device: no remote copies, remote signals or barrier semaphores. Data moves between devices by JAX's collectives and lax.ppermute only.
A program may use at most 128 MiB of HBM per device.

```python
import jax
import jax.numpy as jnp
from jax import lax

QH = 64
KVH = 8
HD = 128
ROWS_DEV = 256
BLOCK = 128
ANCHOR = 128
FINAL = 64
D = 8192
SHARDS = 64
TOKENS = 16384
BLK_DEV = 2
BLOCKS = 128
P_MAX = 32


def draw_queries(key, part):
    noise = 2.5 * jax.random.truncated_normal(jax.random.fold_in(key, 1), -3.2, 3.2, (TOKENS, QH * HD))
    return noise.astype(jnp.bfloat16)


def draw_keys(key, part):
    noise = jax.random.truncated_normal(jax.random.fold_in(key, 2), -6.0, 6.0, (TOKENS, KVH * HD))
    return noise.astype(jnp.bfloat16)


def draw_final_queries(key, part):
    noise = 2.5 * jax.random.truncated_normal(jax.random.fold_in(key, 3), -3.2, 3.2, (FINAL, QH * HD))
    return noise.astype(jnp.bfloat16)


def pass_tables(key):
    base_key = jax.random.fold_in(key, 202)
    key_order, key_block, key_count = jax.random.split(base_key, 3)
    sources = jnp.arange(SHARDS, dtype=jnp.int32)
    noise_rank = jax.random.randint(key_order, (SHARDS, SHARDS), 0, 1 << 20)
    later_source = (sources[None, :] >= sources[:, None]).astype(jnp.int32)
    ranking = noise_rank * SHARDS + sources[None, :] + later_source * (1 << 27)
    source_order = jnp.argsort(ranking, axis=1)[:, :P_MAX].astype(jnp.int32)
    block_pick = jax.random.randint(key_block, (SHARDS, P_MAX), 0, BLK_DEV)
    block_table = source_order * BLK_DEV + block_pick
    reachable = jnp.minimum(sources, P_MAX)
    lowest = (reachable + 1) // 2
    counts = lowest + jax.random.randint(key_count, (SHARDS,), 0, 1 << 20) % (reachable - lowest + 1)
    counts = counts.at[SHARDS - 1].set(P_MAX)
    return (block_table.astype(jnp.int32), counts.astype(jnp.int32))


def draw_pass_list(key, part):
    block_table, counts = pass_tables(key)
    return block_table


def draw_pass_count(key, part):
    block_table, counts = pass_tables(key)
    return counts


def block_scale(stream_key, extent, pieces, smallest, high):
    gain = 1.0
    for axis_at, blocks in pieces:
        steps = jax.random.uniform(jax.random.fold_in(jax.random.fold_in(stream_key, 6), axis_at), (blocks,), jnp.float32, smallest / len(pieces), high / len(pieces))
        gain = gain * jnp.repeat(jnp.exp(steps), extent[axis_at] // blocks).reshape((-1,) + (1,) * (len(extent) - 1 - axis_at))
    return gain


def gaussian(key, extent, deviation, most, pieces=(), held_as=jnp.bfloat16):
    array = jax.random.normal(key, extent, jnp.float32) * deviation
    if len(pieces) > 0:
        array = block_scale(key, extent, pieces, -0.22, 0.18) * array
    return jnp.clip(array, min=-most, max=most).astype(held_as)


def setup_inputs(seed: int = 0) -> dict:
    seeds = jax.random.split(jax.random.key(seed), 10)
    queries = draw_queries(jax.random.fold_in(seeds[9], 71), 0)
    keys = draw_keys(jax.random.fold_in(seeds[9], 71), 0)
    values = gaussian(seeds[2], (TOKENS, KVH * HD), 1.0, 6.0, ((0, 64), (1, 4)))
    pass_list = draw_pass_list(jax.random.fold_in(seeds[9], 71), 0)
    pass_count = draw_pass_count(jax.random.fold_in(seeds[9], 71), 0)
    final_queries = draw_final_queries(jax.random.fold_in(seeds[9], 71), 0)
    final_keys = gaussian(seeds[6], (FINAL, KVH * HD), 1.0, 6.0, ((0, 64), (1, 4)))
    final_values = gaussian(seeds[7], (FINAL, KVH * HD), 1.0, 6.0, ((0, 64), (1, 4)))
    out_weight = gaussian(seeds[8], (D, D), D ** -0.5, 0.0625, ((0, 4), (1, 64)))
    return {"queries": queries, "keys": keys, "values": values, "pass_list": pass_list, "pass_count": pass_count, "final_queries": final_queries, "final_keys": final_keys, "final_values": final_values, "out_weight": out_weight}


negative_big = -1e30


def head_split(matrix, head_count):
    return matrix.reshape(matrix.shape[0], head_count, -1).transpose(1, 0, 2)


def attend(query_heads, key_heads, value_heads, live_mask):
    group_size = query_heads.shape[0] // key_heads.shape[0]
    scaling = query_heads.shape[-1] ** -0.5

    def one_head(head_index):
        query_rows = query_heads[head_index]
        key_rows = key_heads[head_index // group_size]
        value_rows = value_heads[head_index // group_size]
        scores = jnp.dot(query_rows, key_rows.T, preferred_element_type=jnp.float32) * scaling
        scores = jnp.where(live_mask, scores, negative_big)
        highest = jnp.max(scores, axis=1)
        weights = jnp.exp(scores - highest[:, None])
        weight_sum = jnp.sum(weights, axis=1)
        weighted = jnp.dot(weights.astype(jnp.bfloat16), value_rows, preferred_element_type=jnp.float32)
        return highest, weight_sum, weighted

    return lax.map(one_head, jnp.arange(query_heads.shape[0], dtype=jnp.int32))


def first_mask(shard_index, live_count, local_rows, anchor_slots, pass_slots):
    anchor_live = jnp.broadcast_to(shard_index > 0, (anchor_slots * BLOCK,))
    pass_live = jnp.repeat(jnp.arange(pass_slots, dtype=jnp.int32) < live_count, BLOCK)
    row_index = jnp.arange(local_rows, dtype=jnp.int32)
    causal = row_index[None, :] <= row_index[:, None]
    far_live = jnp.concatenate([anchor_live, pass_live])
    far_live = jnp.broadcast_to(far_live[None, :], (local_rows, far_live.shape[0]))
    return jnp.concatenate([far_live, causal], axis=1)


def finish(weighted, weight_sum):
    local_rows = weighted.shape[1]
    normed = (weighted / weight_sum[:, :, None]).astype(jnp.bfloat16)
    return normed.transpose(1, 0, 2).reshape(local_rows, -1)


def reference(queries, keys, values, pass_list, pass_count, final_queries, final_keys, final_values, out_weight):
    columns = keys.shape[1]
    key_blocks = keys.reshape(BLOCKS, BLOCK, columns)
    value_blocks = values.reshape(BLOCKS, BLOCK, columns)
    anchor_slots = ANCHOR // BLOCK
    anchor_ids = jnp.arange(anchor_slots, dtype=jnp.int32)
    pass_slots = pass_list.shape[1]

    def shard_output(shard_index):
        slot_blocks = jnp.concatenate([anchor_ids, pass_list[shard_index].astype(jnp.int32)])
        first_row = (shard_index * ROWS_DEV).astype(jnp.int32)
        key_rows = jnp.concatenate([key_blocks[slot_blocks].reshape(-1, columns), lax.dynamic_slice_in_dim(keys, first_row, ROWS_DEV, 0)])
        value_rows = jnp.concatenate([value_blocks[slot_blocks].reshape(-1, columns), lax.dynamic_slice_in_dim(values, first_row, ROWS_DEV, 0)])
        live_mask = first_mask(shard_index, pass_count[shard_index], ROWS_DEV, anchor_slots, pass_slots)
        query_rows = lax.dynamic_slice_in_dim(queries, first_row, ROWS_DEV, 0)
        highest, weight_sum, weighted = attend(head_split(query_rows, QH), head_split(key_rows, KVH), head_split(value_rows, KVH), live_mask)
        return finish(weighted, weight_sum)

    attn_out = lax.map(shard_output, jnp.arange(SHARDS, dtype=jnp.int32)).reshape(TOKENS, QH * HD)
    key_table = jnp.concatenate([keys, final_keys])
    value_table = jnp.concatenate([values, final_values])
    row_index = jnp.arange(FINAL, dtype=jnp.int32)
    context_live = jnp.zeros((FINAL, TOKENS), jnp.int32) == 0
    live_two = jnp.concatenate([context_live, row_index[None, :] <= row_index[:, None]], axis=1)
    highest, weight_sum, weighted = attend(head_split(final_queries, QH), head_split(key_table, KVH), head_split(value_table, KVH), live_two)
    final_attn = finish(weighted, weight_sum)
    final_out = jnp.dot(final_attn, out_weight, preferred_element_type=jnp.float32).astype(jnp.bfloat16)
    return attn_out, final_out
```

```python
import functools
import math

import jax
import jax.numpy as jnp
from jax import lax
from jax.experimental import pallas as pl
from jax.experimental.pallas import tpu as pltpu
from jax.sharding import PartitionSpec as P

HD = 128
BLOCK = 128
ROWS = 256
SLOTS = 32
SIDE = 4
LINE = 4
HEADS = 4
UNIT = LINE * ROWS + 16
MSG = ROWS + 16
TILE = 4
FULL = SLOTS // TILE
TAIL = 2 + TILE - 1
NEG = -1e30
SCALE = HD**-0.5
TO_EXP2 = SCALE * math.log2(math.e)


def shifted(array, dx, dy, dz):
    pairs = []
    for x in range(SIDE):
        for y in range(SIDE):
            for z in range(SIDE):
                to = ((x + dx) % SIDE * SIDE + (y + dy) % SIDE) * SIDE + (z + dz) % SIDE
                pairs.append(((x * SIDE + y) * SIDE + z, to))
    return lax.ppermute(array, "ctx", pairs)


def along(axis, step):
    return (step, 0, 0) if axis == 0 else (0, step, 0)


def plane_gather(unit, first, second):
    half = UNIT // 2 // 16 * 16
    up = shifted(unit, *along(first, 1))
    down = shifted(unit, *along(first, -1))
    low = shifted(up[:half], *along(first, 1))
    high = shifted(down[half:], *along(first, -1))
    pieces = {0: unit, 1: up, 3: down, 2: jnp.concatenate([low, high])}
    held = {}
    for back, piece in pieces.items():
        ups = shifted(piece, *along(second, 1))
        downs = shifted(piece, *along(second, -1))
        if back in (0, 1):
            far = shifted(ups, *along(second, 1))
        else:
            far = shifted(downs, *along(second, -1))
        held[back, 0], held[back, 1], held[back, 3], held[back, 2] = (piece, ups, downs, far)
    return held


def table_of(held, swap):
    table = jnp.zeros((SIDE * SIDE, UNIT, HD), jnp.bfloat16)
    for (a, b), piece in held.items():
        at = (b * SIDE + a) if swap else (a * SIDE + b)
        table = table.at[at].set(piece)
    return table.reshape(SIDE * SIDE * UNIT, HD)


def attn_kernel(info, q_ref, k_hbm, v_hbm, o_ref, kbuf, vbuf, ktail, vtail, sbuf, ksem, vsem):
    far = info[42]
    tiles = far // TILE
    rest = far - tiles * TILE

    def fetch(offset, kdst, vdst, sem_at):
        rows = pl.ds(pl.multiple_of(offset, 16), BLOCK)
        pltpu.make_async_copy(k_hbm.at[rows], kdst, ksem.at[sem_at]).start()
        pltpu.make_async_copy(v_hbm.at[rows], vdst, vsem.at[sem_at]).start()

    def start_tile(t, _):
        for i in range(TILE):
            dst = pl.ds(i * BLOCK, BLOCK)
            fetch(info[t * TILE + i], kbuf.at[t, dst], vbuf.at[t, dst], t)
        return 0

    for i in range(TAIL):
        if i < 2:
            offset = info[40 + i]
        else:
            offset = jnp.where(i - 2 < rest, info[tiles * TILE + i - 2], info[40])
        dst = pl.ds(i * BLOCK, BLOCK)
        fetch(offset, ktail.at[dst], vtail.at[dst], FULL)
    lax.fori_loop(0, tiles, start_tile, 0)

    width = TILE * BLOCK
    row = lax.broadcasted_iota(jnp.int32, (ROWS, TAIL * BLOCK), 0)
    col = lax.broadcasted_iota(jnp.int32, (ROWS, TAIL * BLOCK), 1)
    live = col <= jnp.where(col < ROWS, row, ROWS + rest * BLOCK - 1)
    nt = (((1,), (1,)), ((), ()))

    def fold(values, op):
        parts = [values[:, i * HD : (i + 1) * HD] for i in range(values.shape[1] // HD)]
        return functools.reduce(op, parts)

    def q_of(h):
        return q_ref[:ROWS, h * HD : (h + 1) * HD]

    def score_tile(h, t):
        s = lax.dot_general(q_of(h), kbuf[t], nt, preferred_element_type=jnp.float32)
        sbuf[h % 2, t] = s
        return fold(s, jnp.maximum)

    def score_tail(h):
        s = lax.dot_general(q_of(h), ktail[...], nt, preferred_element_type=jnp.float32)
        s = jnp.where(live, s, NEG)
        return s, fold(s, jnp.maximum)

    def weigh(s, peak):
        p = jnp.exp2(s * TO_EXP2 - peak)
        return p.astype(jnp.bfloat16), fold(p, jnp.add)

    def wait_for(t, kdst, vdst):
        rows = pl.ds(0, kdst.shape[0])
        pltpu.make_async_copy(k_hbm.at[rows], kdst, ksem.at[t]).wait()
        pltpu.make_async_copy(v_hbm.at[rows], vdst, vsem.at[t]).wait()

    wait_for(FULL, ktail, vtail)
    tail_s, high = score_tail(0)

    def first(t, high):
        wait_for(t, kbuf.at[t], vbuf.at[t])
        return jnp.maximum(high, score_tile(0, t))

    high = lax.fori_loop(0, tiles, first, high)

    for h in range(HEADS):
        peak = jnp.max(high, axis=1, keepdims=True) * TO_EXP2
        p, total = weigh(tail_s, peak)
        acc = jnp.dot(p, vtail[...], preferred_element_type=jnp.float32)
        more = h + 1 < HEADS
        if more:
            tail_s, high = score_tail(h + 1)
        else:
            high = jnp.zeros((ROWS, HD), jnp.float32)

        def step(t, carry, h=h, more=more, peak=peak):
            total, acc, high = carry
            if more:
                high = jnp.maximum(high, score_tile(h + 1, t))
            p, part = weigh(sbuf[h % 2, t], peak)
            acc = acc + jnp.dot(p, vbuf[t], preferred_element_type=jnp.float32)
            return total + part, acc, high

        total, acc, high = lax.fori_loop(0, tiles, step, (total, acc, high))
        out = acc / jnp.sum(total, axis=1, keepdims=True)
        o_ref[:, h * HD : (h + 1) * HD] = out.astype(jnp.bfloat16)


def attention(info, q, k_table, v_table):
    any_spec = pl.BlockSpec(memory_space=pl.ANY)
    vmem = pl.BlockSpec(memory_space=pltpu.VMEM)
    width = TILE * BLOCK
    keys = (2 + 1 + SLOTS * 3 // 4) * BLOCK
    return pl.pallas_call(
        attn_kernel,
        out_shape=jax.ShapeDtypeStruct((ROWS, HEADS * HD), jnp.bfloat16),
        in_specs=[pl.BlockSpec(memory_space=pltpu.SMEM), vmem, any_spec, any_spec],
        out_specs=vmem,
        scratch_shapes=[
            pltpu.VMEM((FULL, width, HD), jnp.bfloat16),
            pltpu.VMEM((FULL, width, HD), jnp.bfloat16),
            pltpu.VMEM((TAIL * BLOCK, HD), jnp.bfloat16),
            pltpu.VMEM((TAIL * BLOCK, HD), jnp.bfloat16),
            pltpu.VMEM((2, FULL, ROWS, width), jnp.float32),
            pltpu.SemaphoreType.DMA((FULL + 1,)),
            pltpu.SemaphoreType.DMA((FULL + 1,)),
        ],
        cost_estimate=pl.CostEstimate(
            flops=4 * HEADS * ROWS * keys * HD,
            bytes_accessed=4 * keys * HD + 4 * ROWS * HEADS * HD,
            transcendentals=HEADS * ROWS * keys,
        ),
    )(info, q, k_table, v_table)


def final_kernel(first_row, q_ref, pos_ref, row_ref, k_ref, v_ref, o_ref, high, total, acc):
    t = pl.program_id(0)

    @pl.when(t == 0)
    def _():
        high[...] = jnp.full_like(high, NEG)
        total[...] = jnp.zeros_like(total)
        acc[...] = jnp.zeros_like(acc)

    s = lax.dot_general(
        q_ref[...], k_ref[0], (((1,), (1,)), ((), ())), preferred_element_type=jnp.float32
    )
    s = jnp.where(pos_ref[...] + first_row[t] <= row_ref[:, :1], s, NEG)
    top = jnp.maximum(high[:, :1], jnp.max(s, axis=1, keepdims=True))
    p = jnp.exp2((s - top) * TO_EXP2)
    shrink = jnp.exp2((high[:, :1] - top) * TO_EXP2)
    total[...] = jnp.broadcast_to(
        total[:, :1] * shrink + jnp.sum(p, axis=1, keepdims=True), total.shape
    )
    high[...] = jnp.broadcast_to(top, high.shape)
    acc[...] = acc[...] * shrink + jnp.dot(
        p.astype(jnp.bfloat16), v_ref[0], preferred_element_type=jnp.float32
    )

    @pl.when(t == pl.num_programs(0) - 1)
    def _():
        o_ref[...] = (acc[...] / total[...]).astype(jnp.bfloat16)


def final_attention(first_row, q, pos, row, k_table, v_table):
    lines = SIDE * SIDE
    rows = q.shape[0]
    return pl.pallas_call(
        final_kernel,
        out_shape=jax.ShapeDtypeStruct((rows, HD), jnp.bfloat16),
        grid=(lines,),
        in_specs=[
            pl.BlockSpec(memory_space=pltpu.SMEM),
            pl.BlockSpec((rows, HD), lambda t: (0, 0)),
            pl.BlockSpec((1, UNIT), lambda t: (0, 0)),
            pl.BlockSpec((rows, HD), lambda t: (0, 0)),
            pl.BlockSpec((1, UNIT, HD), lambda t: (t, 0, 0)),
            pl.BlockSpec((1, UNIT, HD), lambda t: (t, 0, 0)),
        ],
        out_specs=pl.BlockSpec((rows, HD), lambda t: (0, 0)),
        scratch_shapes=[pltpu.VMEM((rows, HD), jnp.float32)] * 3,
        cost_estimate=pl.CostEstimate(
            flops=4 * 128 * lines * UNIT * HD,
            bytes_accessed=4 * lines * UNIT * HD,
            transcendentals=rows * lines * UNIT,
        ),
    )(first_row, q, pos, row, k_table.reshape(lines, UNIT, HD), v_table.reshape(lines, UNIT, HD))


def local(
    queries,
    keys,
    values,
    pass_list,
    pass_count,
    final_queries,
    final_keys,
    final_values,
    out_weight,
):
    ctx = lax.axis_index("ctx")
    my_x, my_y, my_z = ctx // (SIDE * SIDE), ctx // SIDE % SIDE, ctx % SIDE

    listed = jnp.concatenate([pass_list[0], pass_count])
    listed = jnp.pad(listed, (0, HD - listed.shape[0])).astype(jnp.bfloat16)

    def message(main, final, extra):
        rows = [main, final[:, :HD], extra[None, :]]
        return jnp.pad(jnp.concatenate(rows), ((0, MSG - ROWS - 2), (0, 0)))

    none = jnp.zeros((HD,), jnp.bfloat16)
    both = jnp.stack(
        [
            jnp.stack(
                [
                    message(keys[:, at], final_keys[:, at], listed),
                    message(values[:, at], final_values[:, at], none),
                ]
            )
            for at in (slice(0, HD), slice(HD, 2 * HD))
        ]
    )
    q_rows = jnp.pad(jnp.concatenate([queries, final_queries]), ((0, MSG - ROWS - 1), (0, 0)))
    kv_got, q_got = [], []
    for d in range(LINE):
        to = (my_z + d) % LINE
        piece = lax.dynamic_index_in_dim(both, to // 2, 0, keepdims=False)
        kv_got.append(shifted(piece, 0, 0, d) if d else piece)
    for d in range(LINE):
        to = (my_z + d) % LINE
        piece = lax.dynamic_slice_in_dim(q_rows, to * HEADS * HD, HEADS * HD, 1)
        q_got.append(shifted(piece, 0, 0, d) if d else piece)

    def unit_of(part):
        rows = [kv_got[d][part, :ROWS] for d in range(LINE)]
        rows += [kv_got[d][part, ROWS : ROWS + 1] for d in range(LINE)]
        rows.append(jnp.zeros((16 - LINE, HD), jnp.bfloat16))
        return jnp.concatenate(rows)

    k_table = table_of(plane_gather(unit_of(0), 0, 1), False)
    v_table = table_of(plane_gather(unit_of(1), 1, 0), True)

    def offset_of(block):
        shard = block // 2
        back_x = (my_x - shard // (SIDE * SIDE)) % SIDE
        back_y = (my_y - shard // SIDE % SIDE) % SIDE
        back_z = (my_z - shard % SIDE) % LINE
        return (back_x * SIDE + back_y) * UNIT + back_z * ROWS + block % 2 * BLOCK

    infos = []
    for d in range(LINE):
        row = kv_got[d][0, ROWS + 1].astype(jnp.int32)
        shard = ctx - my_z + (my_z - d) % LINE
        blocks = jnp.concatenate(
            [
                jnp.zeros((1,), jnp.int32),
                row[:SLOTS],
                jnp.zeros((7,), jnp.int32),
                2 * shard + jnp.arange(2, dtype=jnp.int32),
            ]
        )
        far = jnp.where(shard > 0, row[SLOTS] + 1, 0)
        infos.append(jnp.concatenate([offset_of(blocks), far[None]]))

    lines = SIDE * SIDE
    unit_row = jnp.arange(UNIT, dtype=jnp.int32)
    back = unit_row - LINE * ROWS
    pos = jnp.where(
        back < 0, -1000, jnp.where(back < LINE, (my_z - back) % LINE, 1000)
    )[None, :]
    step = jnp.arange(lines, dtype=jnp.int32)
    first_row = LINE * ((my_x - step // SIDE) % SIDE * SIDE + (my_y - step % SIDE) % SIDE)
    final_q = jnp.concatenate([q_got[d][ROWS].reshape(HEADS, HD) for d in range(LINE)])
    which = jnp.arange(LINE * HEADS, dtype=jnp.int32) // HEADS
    final_row = ctx - my_z + (my_z - which) % LINE
    final_row = jnp.broadcast_to(final_row[:, None], (LINE * HEADS, HD))
    final_attn = final_attention(first_row, final_q, pos, final_row, k_table, v_table)

    rows = [final_attn[d * HEADS : (d + 1) * HEADS].reshape(1, HEADS * HD) for d in range(LINE)]
    mine = jnp.zeros((LINE, HEADS * HD), jnp.bfloat16)
    for d in range(LINE):
        mine = lax.dynamic_update_slice_in_dim(mine, rows[d], (my_z - d) % LINE, 0)
    part = jnp.zeros((LINE, LINE * HEADS * HD), jnp.bfloat16)
    for d in range(LINE):
        piece = shifted(mine, 0, 0, d) if d else mine
        part = lax.dynamic_update_slice_in_dim(part, piece, (my_z - d) % LINE * HEADS * HD, 1)
    for axis, me in ((1, my_y), (0, my_x)):
        count = part.shape[0]
        wider = jnp.zeros((SIDE * count, part.shape[1]), jnp.bfloat16)
        for d in range(SIDE):
            piece = shifted(part, *along(axis, d)) if d else part
            wider = lax.dynamic_update_slice_in_dim(wider, piece, (me - d) % SIDE * count, 0)
        part = wider
    partial = jnp.dot(part, out_weight, preferred_element_type=jnp.float32).astype(jnp.bfloat16)
    groups = lax.axis_size("head")
    pieces = lax.all_to_all(
        partial.reshape(groups, -1, partial.shape[1]), "head", 0, 0, tiled=True
    )
    final_out = jnp.sum(pieces.astype(jnp.float32), axis=0).astype(jnp.bfloat16)

    attn_out = jnp.zeros((ROWS, LINE * HEADS * HD), jnp.bfloat16)
    for d in (2, 1, 3, 0):
        out = attention(infos[d], q_got[d], k_table, v_table)
        back_to = -d % LINE
        piece = shifted(out, 0, 0, back_to) if d else out
        attn_out = lax.dynamic_update_slice_in_dim(
            attn_out, piece, (my_z - back_to) % LINE * HEADS * HD, 1
        )
    return (attn_out, final_out)


def solution(mesh):
    placed = (
        P("ctx", "head"),
        P("ctx", "head"),
        P("ctx", "head"),
        P("ctx", None),
        P("ctx"),
        P("ctx", "head"),
        P("ctx", "head"),
        P("ctx", "head"),
        P("head", "ctx"),
    )
    return jax.shard_map(
        local,
        mesh=mesh,
        in_specs=placed,
        out_specs=(P("ctx", "head"), P("head", "ctx")),
        check_vma=False,
    )
```

```python
import functools
import math

import jax
import jax.numpy as jnp
from jax import lax
from jax.experimental import pallas as pl
from jax.experimental.pallas import tpu as pltpu
from jax.sharding import PartitionSpec as P

HD = 128
BLOCK = 128
ROWS = 256
SLOTS = 32
SIDE = 4
CORES = 2
LINE = 4
LINES = SIDE * SIDE
HEADS = 4
EXTRA = 16
MSG = ROWS + EXTRA
UNIT = LINE * ROWS + EXTRA
HALF = 528
TILE = 4
FULL = SLOTS // TILE
TAIL = 2 + TILE - 1
VOFF = 64
NEG = -1e30
TO_EXP2 = HD**-0.5 * math.log2(math.e)
NT = (((1,), (1,)), ((), ()))
F32, BF16 = jnp.float32, jnp.bfloat16


def permuted(array, target, back=False):
    pairs = []
    for x in range(SIDE):
        for y in range(SIDE):
            for z in range(SIDE):
                for low in range(2):
                    for core in range(CORES):
                        tx, ty, tz, tc = target(x, y, z, core)
                        one = ((x * SIDE + y) * SIDE + z) * 4 + low * CORES + core
                        two = ((tx * SIDE + ty) * SIDE + tz) * 4 + low * CORES + tc
                        pairs.append((two, one) if back else (one, two))
    return lax.ppermute(array, ("ctx", "head"), pairs)


def round_target(r):
    def target(x, y, z, core):
        g = (z + r) % LINE
        return x, y, 2 * core + g // 2, g % 2

    return target


def plane_target(first, step):
    def target(x, y, z, core):
        if first == (core == 0):
            return (x + step) % SIDE, y, z, core
        return x, (y + step) % SIDE, z, core

    return target


def swapped(array):
    return permuted(array, lambda x, y, z, core: (x, y, z, 1 - core))


VMEM_SPEC = pl.BlockSpec(memory_space=pltpu.VMEM)
SMEM_SPEC = pl.BlockSpec(memory_space=pltpu.SMEM)
ANY_SPEC = pl.BlockSpec(memory_space=pl.ANY)


def extra_rows(rows):
    at = lax.broadcasted_iota(jnp.int32, (EXTRA, HD), 0)
    block = jnp.zeros((EXTRA, HD), F32)
    for i, row in enumerate(rows):
        block = jnp.where(at == i, jnp.broadcast_to(row, (EXTRA, HD)), block)
    return block.astype(BF16)


def pack_kernel(where, k_ref, v_ref, fk_ref, fv_ref, list_ref, o_ref):
    z = where[2]
    listed = list_ref[...].astype(F32)
    for g in range(LINE):
        at = slice(g // 2 * HD, (g // 2 + 1) * HD)
        r = lax.rem(g - z + LINE, LINE)
        if g % 2 == 0:
            o_ref[r, :ROWS] = k_ref[:, at]
            final = fk_ref[:, at].astype(F32)
        else:
            for b in range(ROWS // BLOCK):
                rows = slice(b * BLOCK, (b + 1) * BLOCK)
                o_ref[r, rows] = v_ref[rows, at].astype(F32).T.astype(BF16)
            final = fv_ref[:, at].astype(F32)
        o_ref[r, ROWS:] = extra_rows([final, listed])


def packed(where, keys, values, final_keys, final_values, listed):
    return pl.pallas_call(
        pack_kernel,
        out_shape=jax.ShapeDtypeStruct((LINE, MSG, HD), BF16),
        in_specs=[SMEM_SPEC] + [VMEM_SPEC] * 5,
        out_specs=VMEM_SPEC,
        cost_estimate=pl.CostEstimate(flops=0, bytes_accessed=1 << 20, transcendentals=0),
    )(where, keys, values, final_keys, final_values, listed)


def unit_kernel(where, *refs):
    pieces, o_ref = refs[:LINE], refs[LINE]

    def fill(order):
        for j, r in enumerate(order):
            o_ref[j * ROWS : (j + 1) * ROWS] = pieces[r][:ROWS]
        finals = [pieces[r][ROWS:].astype(F32)[0:1] for r in order]
        o_ref[LINE * ROWS :] = extra_rows(finals)

    @pl.when(where[3] == 0)
    def _():
        fill([0, 1, 2, 3])

    @pl.when(where[3] != 0)
    def _():
        fill([1, 2, 3, 0])


def unit_of(where, pieces):
    return pl.pallas_call(
        unit_kernel,
        out_shape=jax.ShapeDtypeStruct((UNIT, HD), BF16),
        in_specs=[SMEM_SPEC] + [VMEM_SPEC] * LINE,
        out_specs=VMEM_SPEC,
        cost_estimate=pl.CostEstimate(flops=0, bytes_accessed=1 << 20, transcendentals=0),
    )(where, *pieces)


def attn_kernel(info, q_ref, own_hbm, other_hbm, o_ref, kbuf, vbuf, ktail, vtail, sbuf, ksem, vsem):
    far = info[42]
    tiles = far // TILE
    rest = far - tiles * TILE
    core = info[43]

    def fetch(slot, kdst, vdst, sem_at):
        k_rows = pl.ds(pl.multiple_of(info[slot], 16), BLOCK)
        v_rows = pl.ds(pl.multiple_of(info[slot + VOFF], 16), BLOCK)

        @pl.when(core == 0)
        def _():
            pltpu.make_async_copy(own_hbm.at[k_rows], kdst, ksem.at[sem_at]).start()
            pltpu.make_async_copy(other_hbm.at[v_rows], vdst, vsem.at[sem_at]).start()

        @pl.when(core != 0)
        def _():
            pltpu.make_async_copy(other_hbm.at[k_rows], kdst, ksem.at[sem_at]).start()
            pltpu.make_async_copy(own_hbm.at[v_rows], vdst, vsem.at[sem_at]).start()

    def start_tail(i, _):
        left = i - 2
        slot = jnp.where(i < 2, 40 + i, jnp.where(left < rest, tiles * TILE + left, 40))
        dst = pl.ds(pl.multiple_of(i * BLOCK, BLOCK), BLOCK)
        fetch(slot, ktail.at[dst], vtail.at[:, dst], FULL)
        return 0

    def start_tile(i, _):
        t = i // TILE
        dst = pl.ds(pl.multiple_of((i - t * TILE) * BLOCK, BLOCK), BLOCK)
        fetch(i, kbuf.at[t, dst], vbuf.at[t, :, dst], t)
        return 0

    lax.fori_loop(0, TAIL, start_tail, 0)
    lax.fori_loop(0, tiles * TILE, start_tile, 0)

    key = lax.broadcasted_iota(jnp.int32, (TAIL * BLOCK, ROWS), 0)
    row = lax.broadcasted_iota(jnp.int32, (TAIL * BLOCK, ROWS), 1)
    live = key <= jnp.where(key < ROWS, row, ROWS + rest * BLOCK - 1)

    def fold(values, op):
        parts = [values[i * 8 : (i + 1) * 8] for i in range(values.shape[0] // 8)]
        while len(parts) > 1:
            pairs = [op(*parts[i : i + 2]) for i in range(0, len(parts) - 1, 2)]
            parts = pairs + parts[len(pairs) * 2 :]
        return parts[0]

    def scores(keys, h):
        q = q_ref[:ROWS, h * HD : (h + 1) * HD]
        return lax.dot_general(keys, q, NT, preferred_element_type=F32)

    def weigh(s, peak):
        p = jnp.exp2(s * TO_EXP2 - peak)
        return p.astype(BF16), fold(p, jnp.add)

    def wait_for(t, kdst, vdst):
        pltpu.make_async_copy(kdst, kdst, ksem.at[t]).wait()
        pltpu.make_async_copy(vdst, vdst, vsem.at[t]).wait()

    wait_for(FULL, ktail, vtail)
    tails = [jnp.where(live, scores(ktail[...], h), NEG) for h in range(HEADS)]
    highs = tuple(fold(s, jnp.maximum) for s in tails)

    def first(t, highs):
        wait_for(t, kbuf.at[t], vbuf.at[t])
        new = []
        for h, high in enumerate(highs):
            s = scores(kbuf[t], h)
            sbuf[h, t] = s
            new.append(jnp.maximum(high, fold(s, jnp.maximum)))
        return tuple(new)

    highs = lax.fori_loop(0, tiles, first, highs)
    peaks = [jnp.max(high, axis=0, keepdims=True) * TO_EXP2 for high in highs]
    carry = []
    for s, peak in zip(tails, peaks):
        p, total = weigh(s, peak)
        carry.append((total, jnp.dot(vtail[...], p, preferred_element_type=F32)))

    def second(t, carry):
        new = []
        for h, (total, acc) in enumerate(carry):
            p, part = weigh(sbuf[h, t], peaks[h])
            new.append((total + part, acc + jnp.dot(vbuf[t], p, preferred_element_type=F32)))
        return tuple(new)

    carry = lax.fori_loop(0, tiles, second, tuple(carry))
    for h, (total, acc) in enumerate(carry):
        out = acc / jnp.sum(total, axis=0, keepdims=True)
        o_ref[:, h * HD : (h + 1) * HD] = out.T.astype(BF16)


def attention(info, q, own, other):
    width = TILE * BLOCK
    keys = (2 + 1 + SLOTS * 3 // 4) * BLOCK
    return pl.pallas_call(
        attn_kernel,
        out_shape=jax.ShapeDtypeStruct((ROWS, HEADS * HD), BF16),
        in_specs=[SMEM_SPEC, VMEM_SPEC, ANY_SPEC, ANY_SPEC],
        out_specs=VMEM_SPEC,
        scratch_shapes=[
            pltpu.VMEM((FULL, width, HD), BF16),
            pltpu.VMEM((FULL, HD, width), BF16),
            pltpu.VMEM((TAIL * BLOCK, HD), BF16),
            pltpu.VMEM((HD, TAIL * BLOCK), BF16),
            pltpu.VMEM((HEADS, FULL, width, ROWS), F32),
            pltpu.SemaphoreType.DMA((FULL + 1,)),
            pltpu.SemaphoreType.DMA((FULL + 1,)),
        ],
        cost_estimate=pl.CostEstimate(
            flops=8 * HEADS * ROWS * keys * HD,
            bytes_accessed=4 * keys * HD + 4 * ROWS * HEADS * HD,
            transcendentals=HEADS * ROWS * keys,
        ),
    )(info, q, own, other)


def final_kernel(where, q_ref, live_ref, own_hbm, other_hbm, o_ref, k_all, v_all, ksem, vsem):
    core = where[3]

    def start(t, _):
        rows = pl.ds(pl.multiple_of(t * UNIT, 16), UNIT)

        @pl.when(core == 0)
        def _():
            pltpu.make_async_copy(own_hbm.at[rows], k_all.at[t], ksem.at[t]).start()
            pltpu.make_async_copy(other_hbm.at[rows], v_all.at[t], vsem.at[t]).start()

        @pl.when(core != 0)
        def _():
            pltpu.make_async_copy(other_hbm.at[rows], k_all.at[t], ksem.at[t]).start()
            pltpu.make_async_copy(own_hbm.at[rows], v_all.at[t], vsem.at[t]).start()

        return 0

    lax.fori_loop(0, LINES, start, 0)
    context = LINE * ROWS

    def update(carry, s, values):
        high, total, acc = carry
        top = jnp.maximum(high, jnp.max(s, axis=0, keepdims=True))
        p = jnp.exp2((s - top) * TO_EXP2)
        shrink = jnp.exp2((high - top) * TO_EXP2)
        total = total * shrink + jnp.sum(p, axis=0, keepdims=True)
        acc = acc * shrink + jnp.dot(values, p.astype(BF16), preferred_element_type=F32)
        return top, total, acc

    def scores(keys):
        return lax.dot_general(keys, q_ref[...], NT, preferred_element_type=F32)

    def step(t, carry):
        pltpu.make_async_copy(k_all.at[t], k_all.at[t], ksem.at[t]).wait()
        u = lax.rem(t, SIDE) * SIDE + t // SIDE
        pltpu.make_async_copy(v_all.at[u], v_all.at[u], vsem.at[u]).wait()
        values = [v_all[u, i * BLOCK : (i + 1) * BLOCK] for i in range(context // BLOCK)]
        return update(carry, scores(k_all[t, :context]), jnp.concatenate(values, axis=1))

    rows = q_ref.shape[0]
    carry = (jnp.full((1, rows), NEG, F32), jnp.zeros((1, rows), F32), jnp.zeros((HD, rows), F32))
    carry = lax.fori_loop(0, LINES, step, carry)
    extra_k = jnp.concatenate([k_all[t, context:] for t in range(LINES)])
    order = [t % SIDE * SIDE + t // SIDE for t in range(LINES)]
    extra_v = jnp.concatenate([v_all[u, context:] for u in order])
    s = jnp.where(live_ref[...] != 0, scores(extra_k), NEG)
    high, total, acc = update(carry, s, extra_v.astype(F32).T.astype(BF16))
    o_ref[...] = (acc / total).T[: o_ref.shape[0]].astype(BF16)


def final_attention(where, q, live, own, other):
    return pl.pallas_call(
        final_kernel,
        out_shape=jax.ShapeDtypeStruct((LINE * HEADS, HD), BF16),
        in_specs=[SMEM_SPEC, VMEM_SPEC, VMEM_SPEC, ANY_SPEC, ANY_SPEC],
        out_specs=VMEM_SPEC,
        scratch_shapes=[
            pltpu.VMEM((LINES, UNIT, HD), BF16),
            pltpu.VMEM((LINES, UNIT, HD), BF16),
            pltpu.SemaphoreType.DMA((LINES,)),
            pltpu.SemaphoreType.DMA((LINES,)),
        ],
        cost_estimate=pl.CostEstimate(
            flops=4 * 128 * LINES * UNIT * HD,
            bytes_accessed=4 * LINES * UNIT * HD,
            transcendentals=128 * LINES * UNIT,
        ),
    )(where, q, live, own, other)


def plane_gather(unit):
    up, down = permuted(unit, plane_target(True, 1)), permuted(unit, plane_target(True, -1))
    unit_up, unit_down = (permuted(unit, plane_target(False, s)) for s in (1, -1))
    low = permuted(up[:HALF], plane_target(True, 1))
    high = permuted(down[HALF:], plane_target(True, -1))
    rest = jnp.concatenate([up, low, high, down])
    rest_up, rest_down = (permuted(rest, plane_target(False, s)) for s in (1, -1))
    far_up = permuted(jnp.concatenate([unit_up, rest_up[:UNIT]]), plane_target(False, 1))
    far_down = permuted(rest_down[UNIT:], plane_target(False, -1))
    return [
        ((0, 0), unit), ((0, 1), rest),
        ((1, 0), unit_up), ((1, 1), rest_up),
        ((3, 0), unit_down), ((3, 1), rest_down),
        ((2, 0), far_up), ((2, 2), far_down),
    ]


def table_of(pieces):
    table = jnp.zeros((LINES * UNIT, HD), BF16)
    for (second, first), piece in pieces:
        table = lax.dynamic_update_slice_in_dim(table, piece, (second * SIDE + first) * UNIT, 0)
    return table


def local(
    queries,
    keys,
    values,
    pass_list,
    pass_count,
    final_queries,
    final_keys,
    final_values,
    out_weight,
):
    ctx = lax.axis_index("ctx")
    core = lax.axis_index("head") % CORES
    my_x, my_y, my_z = ctx // LINES, ctx // SIDE % SIDE, ctx % SIDE
    where = jnp.stack([my_x, my_y, my_z, core])

    listed = jnp.pad(jnp.concatenate([pass_list[0], pass_count]), (0, HD - SLOTS - 1))[None]
    sent = packed(where, keys, values, final_keys, final_values, listed)
    got = [permuted(sent[r], round_target(r)) for r in range(LINE)]
    q_rows = jnp.pad(jnp.concatenate([queries, final_queries]), ((0, EXTRA - 1), (0, 0)))
    q_got = []
    for r in range(LINE):
        group = (my_z + r) % LINE
        piece = lax.dynamic_slice_in_dim(q_rows, group * HEADS * HD, HEADS * HD, 1)
        q_got.append(permuted(piece, round_target(r)))

    pieces = plane_gather(unit_of(where, got))
    own = table_of(pieces)
    other = table_of([(at, swapped(piece)) for at, piece in pieces])

    def offsets_of(block):
        shard = block // 2
        back_x = (my_x - shard // LINES) % SIDE
        back_y = (my_y - shard // SIDE % SIDE) % SIDE
        slot = (2 * (my_z % 2) - shard % SIDE) % LINE
        inner = slot * ROWS + block % 2 * BLOCK
        return (back_y * SIDE + back_x) * UNIT + inner, (back_x * SIDE + back_y) * UNIT + inner

    def shard_of(r):
        return ctx - my_z + (2 * (my_z % 2) + core - r) % LINE

    infos = []
    for r in range(LINE):
        row = got[r][ROWS + 1].astype(jnp.int32)
        shard = shard_of(r)
        blocks = jnp.concatenate(
            [
                jnp.zeros((1,), jnp.int32),
                row[:SLOTS],
                jnp.zeros((7,), jnp.int32),
                2 * shard + jnp.arange(2, dtype=jnp.int32),
            ]
        )
        far = jnp.where(shard > 0, row[SLOTS] + 1, 0)
        k_at, v_at = offsets_of(blocks)
        gap = jnp.zeros((VOFF - 44,), jnp.int32)
        infos.append(jnp.concatenate([k_at, far[None], core[None], gap, v_at]))

    extra = jnp.arange(LINES * EXTRA, dtype=jnp.int32)
    line = extra // EXTRA
    line_y, line_x = (my_y - line // SIDE) % SIDE, (my_x - line % SIDE) % SIDE
    slot = extra % EXTRA
    key_row = (line_x * SIDE + line_y) * LINE + (2 * (my_z % 2) - slot) % LINE
    key_row = jnp.where(slot < LINE, key_row, 1 << 20)
    query_row = jnp.repeat(jnp.stack([shard_of(r) for r in range(LINE)]), HEADS)
    query_row = jnp.pad(query_row, (0, HD - LINE * HEADS))
    live = (key_row[:, None] <= query_row[None, :]).astype(jnp.int32)
    final_q = jnp.concatenate([q_got[r][ROWS].reshape(HEADS, HD) for r in range(LINE)])
    final_q = jnp.pad(final_q, ((0, HD - LINE * HEADS), (0, 0)))
    final_attn = final_attention(where, final_q, live, own, other)

    mine = jnp.zeros((LINE, HEADS * HD), BF16)
    for r in range(LINE):
        row = final_attn[r * HEADS : (r + 1) * HEADS].reshape(1, HEADS * HD)
        mine = lax.dynamic_update_slice_in_dim(mine, row, shard_of(r) % LINE, 0)
    part = jnp.zeros((LINE, LINE * HEADS * HD), BF16)
    for r in range(LINE):
        piece = permuted(mine, round_target(r), back=True)
        group = (my_z + r) % LINE
        part = lax.dynamic_update_slice_in_dim(part, piece, group * HEADS * HD, 1)
    for axis in (1, 0):
        for bit in (1, 2):

            def target(x, y, z, c, axis=axis, bit=bit):
                return (x ^ bit, y, z, c) if axis == 0 else (x, y ^ bit, z, c)

            count = part.shape[0]
            piece = permuted(part, target)
            odd = (my_y if axis else my_x) // bit % 2
            wider = jnp.zeros((2 * count, part.shape[1]), BF16)
            wider = lax.dynamic_update_slice_in_dim(wider, part, odd * count, 0)
            part = lax.dynamic_update_slice_in_dim(wider, piece, (1 - odd) * count, 0)
    partial = jnp.dot(part, out_weight, preferred_element_type=F32).astype(BF16)
    groups = lax.axis_size("head")
    sums = lax.all_to_all(partial.reshape(groups, -1, partial.shape[1]), "head", 0, 0, tiled=True)
    final_out = jnp.sum(sums.astype(F32), axis=0).astype(BF16)

    attn_out = jnp.zeros((ROWS, LINE * HEADS * HD), BF16)
    for r in range(LINE):
        out = attention(infos[r], q_got[r], own, other)
        piece = permuted(out, round_target(r), back=True)
        group = (my_z + r) % LINE
        attn_out = lax.dynamic_update_slice_in_dim(attn_out, piece, group * HEADS * HD, 1)
    return (attn_out, final_out)


def solution(mesh):
    placed = (
        P("ctx", "head"),
        P("ctx", "head"),
        P("ctx", "head"),
        P("ctx", None),
        P("ctx"),
        P("ctx", "head"),
        P("ctx", "head"),
        P("ctx", "head"),
        P("head", "ctx"),
    )
    return jax.shard_map(
        local,
        mesh=mesh,
        in_specs=placed,
        out_specs=(P("ctx", "head"), P("head", "ctx")),
        check_vma=False,
    )
```
